512 devices in a mesh: req: 128 (over z, x_hi, y), tensor: 4 (over x_lo, core).
Axes of the slice: x: 4 (x_hi: 2, x_lo: 2; x = x_hi * 2 + x_lo), y: 8, z: 8, core: 2. Of those that a mesh axis runs over, the one named last changes fastest.
Arguments:
- tokens: bfloat16 [32768, 2048], P('req'), may hold values from -6 to 6
- segment_ids: int32 [128, 256], P('req'), may hold values from 0 to 7, never falling along the last dimension, each value on 1 to 128 neighbouring positions
- padding: int32 [32768], P('req'), may hold values 0 or 1
- attn_experts: int32 [32768, 2], P('req'), may hold values from 0 to 3, all different within a row
- gain: float32 [2048], replicated, may hold values from 0.1 to 1.9
- w_router: float32 [2048, 4], replicated, may hold values from -0.125 to 0.125
- w_query: bfloat16 [2048, 4096], P('req', 'tensor'), may hold values from -1 to 1
- w_kv: bfloat16 [2048, 2048], P('req', 'tensor'), may hold values from -1 to 1
- w_out: bfloat16 [4096, 2048], P('tensor', 'req'), may hold values from -0.1875 to 0.1875
- page_shift: int32 [16], replicated, may hold values from 0 to 15, as said below
Outputs:
- attended: bfloat16 [32768, 2048], P('req', 'tensor')
- kv_cache: bfloat16 [2048, 16, 2048], P('req', None, 'tensor')
The draws below stay inside these ranges and needn't reach their ends.
Inputs may be any that keep to these rules, and one draw needn't show every extreme that they name: `segment_ids`: segment ids never fall along a batch; each of the 8 prompts holds at least one token and at most 128. `attn_experts`: the two experts of a token differ. Block j of every batch goes to the owner page_shift[j] places further along req, cyclically, into that owner's block j.
All inputs are finite; a program needn't handle non-finite values. No bound on the sum of `padding` on one device may be relied on, other than what follows from the above.
Results may differ from the reference program's by a relative error of at most 0.013.
Values may be sent and summed in bfloat16 or wider, within the bound.
A program may use at most 64 MiB of HBM per device.

```python
import math
import jax
import jax.numpy as jnp
import numpy as np
from jax import lax

D = 2048
HD = 128
HEADS = 8
KVH = 8
EXPERTS = 4
SEGS = 8
PAGE = 16
TOK = 256
SPREAD = 16
BATCHES = 128
TOKENS = 32768
PAGES = 16


def draw_tokens(key, part):
    noise_key = jax.random.fold_in(jax.random.fold_in(key, 1), 0)
    return jnp.clip(jax.random.normal(noise_key, (TOKENS, D), jnp.float32), -6.0, 6.0).astype(jnp.bfloat16)


def draw_w_query(key, part):
    values = jnp.clip(jax.random.normal(jax.random.fold_in(key, 2), (D, HEADS * EXPERTS * HD), jnp.float32), -6.0, 6.0) / math.sqrt(D)
    return values.astype(jnp.bfloat16)


def draw_w_kv(key, part):
    values = jnp.clip(jax.random.normal(jax.random.fold_in(key, 3), (D, KVH * 2 * HD), jnp.float32), -6.0, 6.0) / math.sqrt(D)
    return values.astype(jnp.bfloat16)


def draw_page_shift(key, part):
    value_key, spot_key, other_key = jax.random.split(jax.random.fold_in(key, 11), 3)
    values = jax.random.randint(value_key, (PAGES,), 0, SPREAD)
    spot = jax.random.randint(spot_key, (), 0, PAGES)
    other = (spot + 1 + jax.random.randint(other_key, (), 0, PAGES - 1)) % PAGES
    index = jnp.arange(PAGES, dtype=jnp.int32)
    values = jnp.where(index == spot, SPREAD - 1, values)
    values = jnp.where(index == other, 0, values)
    return values.astype(jnp.int32)


def set_ends(values, stream_key, smallest, largest):
    place = [jax.random.randint(jax.random.fold_in(stream_key, axis), (), 0, length) for axis, length in enumerate(values.shape)]
    longest = values.shape.index(max(values.shape))
    next_to = place[:longest] + [(place[longest] + 1) % values.shape[longest]] + place[longest + 1:]
    return values.at[tuple(place)].set(smallest).at[tuple(next_to)].set(largest)


def shard_levels(stream_key, shape, cuts, low, largest):
    loudness = 1.0
    for dim, blocks in cuts:
        steps = jax.random.uniform(jax.random.fold_in(jax.random.fold_in(stream_key, 6), dim), (blocks,), jnp.float32, low / len(cuts), largest / len(cuts))
        loudness = loudness * jnp.repeat(jnp.exp(steps), shape[dim] // blocks).reshape((-1,) + (1,) * (len(shape) - 1 - dim))
    return loudness


def distinct(stream_key, rows, number_of, top, lift):
    order = jax.random.permutation(jax.random.fold_in(stream_key, 1), number_of)
    boost = order
    for power in range(3):
        boost = boost * boost // number_of
    boost = boost * lift // number_of
    tickets = jax.random.randint(jax.random.fold_in(stream_key, 2), (rows, number_of), 0, 4096) + boost
    fixed_rows = jax.random.permutation(jax.random.fold_in(stream_key, 3), rows)[jnp.arange(number_of) % rows]
    tickets = jnp.where(jnp.arange(rows)[:, None] == fixed_rows[None, :], 1 << 14, tickets)
    merit = tickets * number_of + jnp.arange(number_of)
    return lax.top_k(merit.astype(jnp.int32), top)[1].astype(jnp.int32)


def length_profile(number_of, total, bound, slope):
    loads = [(1 << 20) // math.isqrt(grade ** slope) + 1 for grade in range(2, number_of + 1)]
    spare, given = total - bound - (number_of - 1), [1] * (number_of - 1)
    while spare > 0:
        movable = [i for i in range(number_of - 1) if given[i] < bound]
        whole, left = sum([loads[i] for i in movable]), spare
        for i in movable:
            extra = min(bound - given[i], max(1, left * loads[i] // whole), spare)
            given[i] = given[i] + extra
            spare = spare - extra
    return np.array([bound] + given)


def ragged_sizes(own_key, number_of, total, bound, slope):
    if number_of == 2:
        one = jax.random.randint(own_key, (), max(1, total - bound), min(bound, total - 1) + 1)
        return jnp.stack([one, total - one])
    lengths = jnp.asarray(length_profile(number_of, total, bound, slope), jnp.int32)
    couples = (number_of - 1) // 2
    source_of, sink = lengths[1:1 + 2 * couples:2], lengths[2:2 + 2 * couples:2]
    margin = jnp.minimum(source_of - 1, bound - sink)
    shifted = jax.random.randint(jax.random.fold_in(own_key, 1), (couples,), 0, 1 << 20) % (margin + 1)
    lengths = lengths.at[1:1 + 2 * couples:2].set(source_of - shifted).at[2:2 + 2 * couples:2].set(sink + shifted)
    return lengths[jax.random.permutation(jax.random.fold_in(own_key, 2), number_of)]


def bell_draw(stream_key, dims, deviation, reach, shards=(), kind=jnp.bfloat16):
    array = jax.random.normal(stream_key, dims, jnp.float32) * deviation
    if len(shards) > 0:
        array = shard_levels(stream_key, dims, shards, -0.22, 0.18) * array
    return jnp.clip(array, min=-reach, max=reach).astype(kind)


def setup_inputs(seed: int = 0) -> dict:
    seeds = jax.random.split(jax.random.key(seed), 11)
    return {
        "tokens": draw_tokens(jax.random.fold_in(seeds[10], 71), 0),
        "segment_ids": jax.vmap(lambda own: jnp.searchsorted(jnp.cumsum(ragged_sizes(own, SEGS, TOK, TOK // 2, 2)), jnp.arange(TOK), side="right"))(jax.random.split(seeds[1], BATCHES)).reshape((BATCHES, TOK)).astype(jnp.int32),
        "padding": set_ends((jax.random.randint(seeds[2], (TOKENS,), 0, 8) < 7).astype(jnp.int32), jax.random.fold_in(seeds[2], 1), 0, 1),
        "attn_experts": distinct(seeds[3], TOKENS, EXPERTS, 2, 4096),
        "gain": jnp.clip(1.0 + 0.18 * jax.random.normal(seeds[4], (D,), jnp.float32), 0.1, 1.9),
        "w_router": bell_draw(seeds[5], (D, EXPERTS), D ** -0.5, 0.125, (), jnp.float32),
        "w_query": draw_w_query(jax.random.fold_in(seeds[10], 71), 0),
        "w_kv": draw_w_kv(jax.random.fold_in(seeds[10], 71), 0),
        "w_out": bell_draw(seeds[8], (HEADS * EXPERTS * HD, D), (HEADS * HD) ** -0.5, 0.1875, ((0, 4), (1, 128))),
        "page_shift": draw_page_shift(jax.random.fold_in(seeds[10], 71), 0),
    }


def rotate(values, position):
    half_size = values.shape[-1] // 2
    freqs = 10000.0 ** (-jnp.arange(half_size, dtype=jnp.float32) / half_size)
    angles = position.astype(jnp.float32)[:, None] * freqs[None, :]
    angles = angles.reshape((values.shape[0],) + (1,) * (values.ndim - 2) + (half_size,))
    cosine = jnp.cos(angles)
    sine = jnp.sin(angles)
    first = values[..., :half_size]
    second = values[..., half_size:]
    return jnp.concatenate([first * cosine - second * sine, second * cosine + first * sine], axis=-1)

def one_batch(packed, gain, w_router, w_query, w_kv, w_out):
    x_rows, seg_row, pad_row, expert_row = packed
    count = x_rows.shape[0]
    starts = lax.optimization_barrier(jnp.sum((seg_row[None, :] < seg_row[:, None]).astype(jnp.int32), axis=1))
    position = jnp.arange(count, dtype=jnp.int32) - starts
    x_float = x_rows.astype(jnp.float32)
    normed = (x_float * lax.rsqrt(lax.optimization_barrier(jnp.mean(x_float * x_float, axis=1, keepdims=True)) + 1e-06) * gain[None, :]).astype(jnp.bfloat16)
    pad_float = pad_row.astype(jnp.float32)
    keyval = jnp.dot(normed, w_kv, preferred_element_type=jnp.float32).reshape(count, KVH, 2, HD)
    keys = rotate(keyval[:, :, 0, :], position)
    keyval = jnp.stack([keys, keyval[:, :, 1, :]], axis=2) * pad_float[:, None, None, None]
    keyval = keyval.astype(jnp.bfloat16)
    logits = jnp.dot(normed.astype(jnp.float32), w_router, preferred_element_type=jnp.float32)
    selector = (expert_row[:, :, None] == jnp.arange(EXPERTS, dtype=jnp.int32)[None, None, :]).astype(jnp.float32)
    gates = jnp.einsum('tse,te->ts', selector, jax.nn.sigmoid(logits))
    query_all = jnp.dot(normed, w_query, preferred_element_type=jnp.float32).reshape(count, HEADS, EXPERTS, HD)
    query_all = rotate(query_all, position)
    queries = jnp.einsum('thed,tse->tshd', query_all, selector).astype(jnp.bfloat16)
    keys_b = keyval[:, :, 0, :].astype(jnp.float32)
    values_b = keyval[:, :, 1, :].astype(jnp.float32)
    scores = jnp.einsum('tshd,uhd->shtu', queries.astype(jnp.float32), keys_b) / jnp.sqrt(jnp.float32(HD))
    index = jnp.arange(count, dtype=jnp.int32)
    allowed = (seg_row[:, None] == seg_row[None, :]) & (index[None, :] <= index[:, None])
    allowed = allowed & ((pad_row[None, :] == 1) | (index[None, :] == index[:, None]))
    masked = jnp.where(allowed[None, None], scores, -1e+30)
    peak = lax.optimization_barrier(jnp.max(masked, axis=3, keepdims=True))
    weights = jnp.where(allowed[None, None], jnp.exp(masked - peak), 0.0)
    total = lax.optimization_barrier(jnp.sum(weights, axis=3))
    weights_b = weights.astype(jnp.bfloat16).astype(jnp.float32)
    heads_out = jnp.einsum('shtu,uhd->tshd', weights_b, values_b) / jnp.transpose(total, (2, 0, 1))[:, :, :, None]
    mixed = jnp.einsum('tshd,tse->thed', heads_out * gates[:, :, None, None], selector) * pad_float[:, None, None, None]
    mixed = mixed.reshape(count, HEADS * EXPERTS * HD).astype(jnp.bfloat16)
    attended = jnp.dot(mixed, w_out, preferred_element_type=jnp.float32).astype(jnp.bfloat16)
    return (attended, keyval.reshape(PAGES, PAGE, KVH * 2 * HD))

def reference(tokens, segment_ids, padding, attn_experts, gain, w_router, w_query, w_kv, w_out, page_shift):
    packed = (tokens.reshape(BATCHES, TOK, D), segment_ids, padding.reshape(BATCHES, TOK), attn_experts.reshape(BATCHES, TOK, 2))
    attended, pages = lax.map(lambda item: one_batch(item, gain, w_router, w_query, w_kv, w_out), packed)
    source = (jnp.arange(BATCHES, dtype=jnp.int32)[:, None] - page_shift[None, :]) % BATCHES
    cache = pages[source, jnp.arange(PAGES, dtype=jnp.int32)[None, :]]
    return (attended.reshape(TOKENS, D), cache.reshape(BATCHES * PAGES, PAGE, KVH * 2 * HD))
```

```python
import jax
import jax.numpy as jnp
from jax import lax
from jax.experimental import pallas as pl
from jax.experimental.pallas import tpu as pltpu
from jax.sharding import PartitionSpec as P

HD = 128
EXPERTS = 4
BITS = 4
MESH = pl.DeviceIdType.MESH
RING = 8
PAIR = 2


def place(z, x, y):
    return {"req": ((z + RING) % RING * PAIR + x) * RING + (y + RING) % RING}


def gather_kernel(shard_ref, full_ref, local_sem, swap_sems, send_sems, recv_sems):
    me = lax.axis_index("req")
    z, x, y = me // (PAIR * RING), me // RING % PAIR, me % RING
    partner = place(z, 1 - x, y)
    around = {
        ("z", 1): place(z + 1, x, y),
        ("z", -1): place(z - 1, x, y),
        ("y", 1): place(z, x, y + 1),
        ("y", -1): place(z, x, y - 1),
    }
    barrier = pltpu.get_barrier_semaphore()
    for device in [partner] + list(around.values()):
        pl.semaphore_signal(barrier, inc=1, device_id=device, device_id_type=MESH)
    pl.semaphore_wait(barrier, 5)

    keep = pltpu.make_async_copy(shard_ref, full_ref.at[z, x, y], local_sem)
    keep.start()
    swap = pltpu.make_async_remote_copy(
        src_ref=shard_ref,
        dst_ref=full_ref.at[z, x, y],
        send_sem=swap_sems.at[0],
        recv_sem=swap_sems.at[1],
        device_id=partner,
        device_id_type=MESH,
    )
    swap.start()

    issued = []

    def send(axis, way, block):
        slot = len(issued)
        copy = pltpu.make_async_remote_copy(
            src_ref=block,
            dst_ref=block,
            send_sem=send_sems.at[slot],
            recv_sem=recv_sems.at[slot],
            device_id=around[axis, way],
            device_id_type=MESH,
        )
        copy.start()
        issued.append(copy)
        return copy

    half = RING // 2

    def one(axis, way, step, _):
        back = (-way) * step + RING
        if axis == "z":
            return full_ref.at[(z + back) % RING, 0, y]
        return full_ref.at[z, 1, (y + back) % RING]

    def many(axis, way, step, chunk):
        back = (-way) * step + RING
        if axis == "y":
            return full_ref.at[pl.ds(half * chunk, half), 0, (y + back) % RING]
        return full_ref.at[(z + back) % RING, 1, pl.ds(half * chunk, half)]

    def rounds(block, lanes):
        flying = {}
        for step in range(half):
            for lane in lanes:
                axis, way, chunk, hops = lane
                if step < hops:
                    if step > 0:
                        flying[lane].wait_recv()
                    flying[lane] = send(axis, way, block(axis, way, step, chunk))
        for lane in lanes:
            flying[lane].wait_recv()

    keep.wait()
    swap.wait()
    rounds(one, [(axis, way, 0, half if way == 1 else half - 1) for way in (1, -1) for axis in ("z", "y")])
    rounds(
        many,
        [
            (axis, way, chunk, half if (way == 1) == (chunk == 0) else half - 1)
            for chunk in (0, 1)
            for way in (1, -1)
            for axis in ("z", "y")
        ],
    )
    for copy in issued:
        copy.wait_send()


def gather_all(shard):
    rows, columns = shard.shape
    sends = 4 * RING + 4 * (RING // 2) - 6
    full = pl.pallas_call(
        gather_kernel,
        out_shape=jax.ShapeDtypeStruct((RING, PAIR, RING, rows, columns), shard.dtype),
        in_specs=[pl.BlockSpec(memory_space=pl.ANY)],
        out_specs=pl.BlockSpec(memory_space=pl.ANY),
        scratch_shapes=[
            pltpu.SemaphoreType.DMA,
            pltpu.SemaphoreType.DMA((2,)),
            pltpu.SemaphoreType.DMA((sends,)),
            pltpu.SemaphoreType.DMA((sends,)),
        ],
        compiler_params=pltpu.CompilerParams(collective_id=0, has_side_effects=True),
        name="gather_weights",
    )(shard)
    return full.reshape(RING * PAIR * RING * rows, columns)


def from_behind(value, axis, steps):
    count = lax.axis_size(axis)
    pairs = [(source, (source + steps) % count) for source in range(count)]
    return lax.ppermute(value, axis, pairs)


def rotate(values, position):
    half_size = values.shape[-1] // 2
    freqs = 10000.0 ** (-jnp.arange(half_size, dtype=jnp.float32) / half_size)
    angles = position.astype(jnp.float32)[:, None] * freqs[None, :]
    angles = angles.reshape((values.shape[0],) + (1,) * (values.ndim - 2) + (half_size,))
    cosine = jnp.cos(angles)
    sine = jnp.sin(angles)
    first = values[..., :half_size]
    second = values[..., half_size:]
    return jnp.concatenate(
        [first * cosine - second * sine, second * cosine + first * sine], axis=-1
    )


def allowed_mask(seg_row, pad_row, query_index, key_index):
    allowed = (seg_row[query_index][:, None] == seg_row[key_index][None, :]) & (
        key_index[None, :] <= query_index[:, None]
    )
    return allowed & (
        (pad_row[key_index][None, :] == 1) | (key_index[None, :] == query_index[:, None])
    )


def attend_dense(queries, keys, values, seg_row, pad_row):
    count = queries.shape[0]
    index = jnp.arange(count, dtype=jnp.int32)
    allowed = allowed_mask(seg_row, pad_row, index, index)
    scores = jnp.einsum(
        "tshd,uhd->shtu", queries, keys, preferred_element_type=jnp.float32
    ) / jnp.sqrt(jnp.float32(queries.shape[-1]))
    masked = jnp.where(allowed[None, None], scores, -1e30)
    peak = jnp.max(masked, axis=3, keepdims=True)
    weights = jnp.where(allowed[None, None], jnp.exp(masked - peak), 0.0)
    total = jnp.sum(weights, axis=3)
    summed = jnp.einsum(
        "shtu,uhd->tshd", weights.astype(jnp.bfloat16), values, preferred_element_type=jnp.float32
    )
    return summed / jnp.transpose(total, (2, 0, 1))[:, :, :, None]


def on_device(
    tokens, segment_ids, padding, attn_experts, gain, w_router, w_query, w_kv, w_out, page_shift
):
    count = tokens.shape[0]
    seg_row = segment_ids[0]
    starts = jnp.sum((seg_row[None, :] < seg_row[:, None]).astype(jnp.int32), axis=1)
    position = jnp.arange(count, dtype=jnp.int32) - starts
    x_float = tokens.astype(jnp.float32)
    normed = (
        x_float
        * lax.rsqrt(jnp.mean(x_float * x_float, axis=1, keepdims=True) + 1e-06)
        * gain[None, :]
    ).astype(jnp.bfloat16)
    pad_float = padding.astype(jnp.float32)
    local_heads = w_kv.shape[1] // (2 * HD)

    weights = gather_all(jnp.concatenate([w_kv, w_query, w_out.T], axis=1))
    kv_columns, query_columns = w_kv.shape[1], w_query.shape[1]

    def add_rows(piece):
        return jnp.dot(normed, piece, preferred_element_type=jnp.float32)

    keyval = add_rows(weights[:, :kv_columns])
    query_all = add_rows(weights[:, kv_columns : kv_columns + query_columns])
    keyval = keyval.reshape(count, local_heads, 2, HD)
    keys_rot = rotate(keyval[:, :, 0, :], position)
    keyval = (
        jnp.stack([keys_rot, keyval[:, :, 1, :]], axis=2) * pad_float[:, None, None, None]
    ).astype(jnp.bfloat16)
    logits = jnp.dot(normed.astype(jnp.float32), w_router, preferred_element_type=jnp.float32)
    selector = (
        attn_experts[:, :, None] == jnp.arange(EXPERTS, dtype=jnp.int32)[None, None, :]
    ).astype(jnp.float32)
    gates = jnp.einsum("tse,te->ts", selector, jax.nn.sigmoid(logits))
    query_all = rotate(query_all.reshape(count, local_heads, EXPERTS, HD), position)
    queries = jnp.einsum("thed,tse->tshd", query_all, selector).astype(jnp.bfloat16)
    keys_b = keyval[:, :, 0, :]
    values_b = keyval[:, :, 1, :]
    heads_out = attend_dense(queries, keys_b, values_b, seg_row, padding)
    mixed = (
        jnp.einsum("tshd,tse->thed", heads_out * gates[:, :, None, None], selector)
        * pad_float[:, None, None, None]
    )
    mixed = mixed.reshape(count, local_heads * EXPERTS * HD).astype(jnp.bfloat16)
    partial_out = lax.dot_general(
        mixed,
        weights[:, kv_columns + query_columns :],
        (((1,), (1,)), ((), ())),
        preferred_element_type=jnp.float32,
    )
    attended = lax.psum_scatter(
        partial_out.astype(jnp.bfloat16), "tensor", scatter_dimension=1, tiled=True
    )
    page_count = page_shift.shape[0]
    page_size = count // page_count
    pages = keyval.reshape(page_count, page_size, local_heads * 2 * HD)
    for level in range(BITS):
        moved = from_behind(pages, "req", 2**level)
        taken = page_shift // 2**level % 2 == 1
        pages = jnp.where(taken[:, None, None], moved, pages)
    return (attended, pages)


def solution(mesh):
    placed = (
        P("req", None),
        P("req", None),
        P("req"),
        P("req", None),
        P(),
        P(),
        P("req", "tensor"),
        P("req", "tensor"),
        P("tensor", "req"),
        P(),
    )
    return jax.shard_map(
        on_device,
        mesh=mesh,
        in_specs=placed,
        out_specs=(P("req", "tensor"), P("req", None, "tensor")),
        check_vma=False,
    )
```

```python
import functools

import jax
import jax.numpy as jnp
from jax import lax
from jax.experimental import pallas as pl
from jax.experimental.pallas import tpu as pltpu
from jax.sharding import PartitionSpec as P

HD = 128
EXPERTS = 4
SLOTS = 2
BITS = 4
MESH = pl.DeviceIdType.MESH
RING = 8
PAIR = 2
CORES = 2
HALF = RING // 2
REQ = RING * PAIR * RING
F32 = jnp.float32
BF16 = jnp.bfloat16


def place(z, x, y):
    return {"req": ((z + RING) % RING * PAIR + x) * RING + (y + RING) % RING}


def layer_kernel(
    parts,
    heads,
    tokens_ref,
    gain_ref,
    router_ref,
    cols_ref,
    rows_ref,
    cos_ref,
    sin_ref,
    shard_ref,
    attended_ref,
    cache_ref,
    full_ref,
    normed_ref,
    bias_ref,
    gates_ref,
    stages_ref,
    inbox_ref,
    query_ref,
    mixed_ref,
    pair_out_ref,
    pair_in_ref,
    far_out_ref,
    far_in_ref,
    local_sem,
    swap_sems,
    send_sems,
    recv_sems,
    page_sems,
    reduce_sems,
):
    count = tokens_ref.shape[0]
    me = lax.axis_index("req")
    z, x, y = me // (PAIR * RING), me // RING % PAIR, me % RING
    mine = lax.axis_index("tensor")
    low, core = mine // CORES, mine % CORES
    partner = place(z, 1 - x, y)
    core_mate = {"tensor": low * CORES + (1 - core)}
    far_mate = {"tensor": (1 - low) * CORES + core}
    around = {
        ("z", 1): place(z + 1, x, y),
        ("z", -1): place(z - 1, x, y),
        ("y", 1): place(z, x, y + 1),
        ("y", -1): place(z, x, y - 1),
    }
    levels = [2**level for level in reversed(range(BITS))]
    ahead = [{"req": (me + shift) % REQ} for shift in levels]
    behind = [{"req": (me + REQ - shift) % REQ} for shift in levels]

    barrier = pltpu.get_barrier_semaphore()
    greeted = [partner, core_mate, far_mate] + list(around.values()) + ahead + behind
    for device in greeted:
        pl.semaphore_signal(barrier, inc=1, device_id=device, device_id_type=MESH)
    pl.semaphore_wait(barrier, len(greeted))

    def remote(src, dst, send_sem, recv_sem, device):
        copy = pltpu.make_async_remote_copy(
            src_ref=src,
            dst_ref=dst,
            send_sem=send_sem,
            recv_sem=recv_sem,
            device_id=device,
            device_id_type=MESH,
        )
        copy.start()
        return copy

    keep = pltpu.make_async_copy(shard_ref, full_ref.at[z, x, y], local_sem)
    keep.start()
    swap = remote(shard_ref, full_ref.at[z, x, y], swap_sems.at[0], swap_sems.at[1], partner)
    issued = []

    def send(axis, way, block):
        slot = len(issued)
        copy = remote(block, block, send_sems.at[slot], recv_sems.at[slot], around[axis, way])
        issued.append(copy)
        return copy

    def single(axis, way, step):
        back = (-way) * step + RING
        if axis == "z":
            return full_ref.at[(z + back) % RING, 0, y]
        return full_ref.at[z, 1, (y + back) % RING]

    def several(axis, way, step, part, chunk):
        back = (-way) * step + RING
        columns = pl.ds(*parts[part])
        run = pl.ds(HALF * chunk, HALF)
        if axis == "y":
            return full_ref.at[run, 0, (y + back) % RING, :, columns]
        return full_ref.at[(z + back) % RING, 1, run, :, columns]

    flying = {}
    streams = [(axis, way) for way in (1, -1) for axis in ("z", "y")]

    def first_round(step):
        for axis, way in streams:
            if step < (HALF if way == 1 else HALF - 1):
                if step > 0:
                    flying[axis, way].wait_recv()
                flying[axis, way] = send(axis, way, single(axis, way, step))

    def first_end():
        for stream in streams:
            flying[stream].wait_recv()

    def turn(part, step, chunk):
        for axis, way in streams:
            if step < (HALF if (way == 1) == (chunk == 0) else HALF - 1):
                lane = (axis, way, part, chunk)
                if step > 0:
                    flying[lane].wait_recv()
                flying[lane] = send(axis, way, several(axis, way, step, part, chunk))

    def arrived(part):
        for chunk in (0, 1):
            for axis, way in streams:
                flying[axis, way, part, chunk].wait_recv()

    def column(index):
        return cols_ref[:, index : index + 1]

    def rotate(values):
        return values * cos_ref[...] + pltpu.roll(values, HD // 2, 1) * sin_ref[...]

    def norm():
        block = 32
        for row in range(0, count, block):
            x_float = tokens_ref[row : row + block, :].astype(F32)
            scale = lax.rsqrt(jnp.mean(x_float * x_float, axis=1, keepdims=True) + 1e-06)
            normed_ref[row : row + block, :] = (x_float * scale * gain_ref[...]).astype(BF16)

    def route():
        logits = jnp.dot(normed_ref[...], router_ref[...], preferred_element_type=F32)
        for slot in range(SLOTS):
            expert = column(2 + slot)
            logit = jnp.zeros((count, 1), F32)
            for index in range(EXPERTS):
                logit = logit + jnp.where(expert == index, logits[:, index : index + 1], 0.0)
            gate = 1.0 / (1.0 + jnp.exp(-logit))
            gates_ref[slot] = jnp.broadcast_to(gate * column(1).astype(F32), (count, HD))

    def mask():
        query_index = lax.broadcasted_iota(jnp.int32, (count, count), 0)
        key_index = lax.broadcasted_iota(jnp.int32, (count, count), 1)
        same = (column(0) == rows_ref[0:1, :]) & (key_index <= query_index)
        allowed = same & ((rows_ref[1:2, :] == 1) | (key_index == query_index))
        bias_ref[...] = jnp.where(allowed, 0.0, -1e30)

    def weights_of(first, size):
        block = full_ref[:, :, :, :, first : first + size]
        return block.reshape(REQ * block.shape[3], size)

    def project_keys():
        first, size = parts[0]
        keyval = jnp.dot(normed_ref[...], weights_of(first, size), preferred_element_type=F32)
        padded = column(1).astype(F32)
        for head in range(heads):
            at = head * 2 * HD
            stages_ref[0, :, at : at + HD] = (rotate(keyval[:, at : at + HD]) * padded).astype(BF16)
            stages_ref[0, :, at + HD : at + 2 * HD] = (
                keyval[:, at + HD : at + 2 * HD] * padded
            ).astype(BF16)

    moves = []

    def page_send(level):
        moves.append(
            remote(
                stages_ref.at[level],
                inbox_ref.at[level],
                page_sems.at[0, level],
                page_sems.at[1, level],
                ahead[level],
            )
        )

    def page_take(level):
        moves[level].wait_recv()
        taken = column(4) // levels[level] % 2 == 1
        chosen = jnp.where(
            taken, inbox_ref[level].astype(F32), stages_ref[level].astype(F32)
        ).astype(BF16)
        if level == BITS - 1:
            cache_ref[...] = chosen
        else:
            stages_ref[level + 1] = chosen

    def project_queries(head):
        size = EXPERTS * HD
        every = jnp.dot(
            normed_ref[...], weights_of(parts[1][0] + head * size, size), preferred_element_type=F32
        )
        for slot in range(SLOTS):
            expert = column(2 + slot)
            chosen = jnp.zeros((count, HD), F32)
            for index in range(EXPERTS):
                chosen = chosen + jnp.where(
                    expert == index, every[:, index * HD : (index + 1) * HD], 0.0
                )
            query_ref[head * SLOTS + slot] = rotate(chosen).astype(BF16)

    def attend(head):
        at = head * 2 * HD
        keys = stages_ref[0, :, at : at + HD]
        values = stages_ref[0, :, at + HD : at + 2 * HD]
        outs = []
        for slot in range(SLOTS):
            scores = lax.dot_general(
                query_ref[head * SLOTS + slot],
                keys,
                (((1,), (1,)), ((), ())),
                preferred_element_type=F32,
            )
            masked = scores * (HD**-0.5) + bias_ref[...]
            weights = jnp.exp(masked - jnp.max(masked, axis=1, keepdims=True))
            total = jnp.sum(weights, axis=1, keepdims=True)
            summed = jnp.dot(weights.astype(BF16), values, preferred_element_type=F32)
            outs.append(summed / total * gates_ref[slot])
        for index in range(EXPERTS):
            mix = jnp.zeros((count, HD), F32)
            for slot in range(SLOTS):
                mix = mix + jnp.where(column(2 + slot) == index, outs[slot], 0.0)
            first = (head * EXPERTS + index) * HD
            mixed_ref[:, first : first + HD] = mix.astype(BF16)

    def project_out(owner):
        span = RING // (PAIR * CORES)
        first, size = parts[2]
        block = full_ref[pl.ds(owner * span, span), :, :, :, first : first + size]
        return lax.dot_general(
            mixed_ref[...],
            block.reshape(span * PAIR * RING * block.shape[3], size),
            (((1,), (1,)), ((), ())),
            preferred_element_type=F32,
        )

    norm()
    keep.wait()
    swap.wait()
    first_round(0)
    mask()
    first_round(1)
    route()
    for step in (2, 3):
        first_round(step)
    first_end()
    for step in range(HALF):
        for chunk in (0, 1):
            turn(0, step, chunk)
    turn(1, 0, 0)
    turn(1, 0, 1)
    arrived(0)
    project_keys()
    page_send(0)
    for step in range(1, HALF):
        for chunk in (0, 1):
            turn(1, step, chunk)
    page_take(0)
    page_send(1)
    turn(2, 0, 0)
    turn(2, 0, 1)
    arrived(1)
    project_queries(0)
    turn(2, 1, 0)
    project_queries(1)
    turn(2, 1, 1)
    page_take(1)
    page_send(2)
    turn(2, 2, 0)
    attend(0)
    turn(2, 2, 1)
    attend(1)
    turn(2, 3, 0)
    turn(2, 3, 1)
    page_take(2)
    page_send(3)
    arrived(2)

    def pair_send(index, owner):
        pair_out_ref[index] = project_out(owner).astype(BF16)
        return remote(
            pair_out_ref.at[index],
            pair_in_ref.at[index],
            reduce_sems.at[0, index],
            reduce_sems.at[1, index],
            core_mate,
        )

    pairs = [pair_send(0, (1 - low) * CORES + (1 - core))]
    far = project_out((1 - low) * CORES + core)
    pairs[0].wait_recv()
    far_out_ref[...] = (far + pair_in_ref[0].astype(F32)).astype(BF16)
    far_copy = remote(far_out_ref, far_in_ref, reduce_sems.at[0, 2], reduce_sems.at[1, 2], far_mate)
    pairs.append(pair_send(1, low * CORES + (1 - core)))
    near = project_out(low * CORES + core)
    pairs[1].wait_recv()
    near = near + pair_in_ref[1].astype(F32)
    page_take(3)
    far_copy.wait_recv()
    attended_ref[...] = (near + far_in_ref[...].astype(F32)).astype(BF16)

    for copy in issued + moves + pairs + [far_copy]:
        copy.wait_send()


def on_device(
    tokens, segment_ids, padding, attn_experts, gain, w_router, w_query, w_kv, w_out, page_shift
):
    count, width = tokens.shape
    seg_row = segment_ids[0]
    starts = jnp.sum((seg_row[None, :] < seg_row[:, None]).astype(jnp.int32), axis=1)
    position = jnp.arange(count, dtype=jnp.int32) - starts
    half_size = HD // 2
    freqs = 10000.0 ** (-jnp.arange(half_size, dtype=F32) / half_size)
    angles = position.astype(F32)[:, None] * freqs[None, :]
    cosine, sine = jnp.cos(angles), jnp.sin(angles)
    cosine = jnp.concatenate([cosine, cosine], axis=1)
    sine = jnp.concatenate([-sine, sine], axis=1)
    shifts = jnp.repeat(page_shift, count // page_shift.shape[0])
    cols = jnp.stack([seg_row, padding, attn_experts[:, 0], attn_experts[:, 1], shifts], axis=1)
    rows = jnp.stack([seg_row, padding], axis=0)
    router = jnp.pad(w_router, ((0, 0), (0, HD - EXPERTS))).astype(BF16)
    shard = jnp.concatenate([w_kv, w_query, w_out.T], axis=1)
    kv_size, query_size, out_size = w_kv.shape[1], w_query.shape[1], w_out.shape[0]
    parts = ((0, kv_size), (kv_size, query_size), (kv_size + query_size, out_size))
    heads = kv_size // (2 * HD)
    slab = width // (PAIR * CORES)
    sends = (4 * HALF - 2) + 3 * (8 * HALF - 4)
    vmem = pl.BlockSpec(memory_space=pltpu.VMEM)
    attended, cache = pl.pallas_call(
        functools.partial(layer_kernel, parts, heads),
        out_shape=(
            jax.ShapeDtypeStruct((count, slab), BF16),
            jax.ShapeDtypeStruct((count, kv_size), BF16),
        ),
        in_specs=[vmem] * 7 + [pl.BlockSpec(memory_space=pl.ANY)],
        out_specs=(vmem, vmem),
        scratch_shapes=[
            pltpu.VMEM((RING, PAIR, RING) + shard.shape, BF16),
            pltpu.VMEM((count, width), BF16),
            pltpu.VMEM((count, count), F32),
            pltpu.VMEM((SLOTS, count, HD), F32),
            pltpu.VMEM((BITS, count, kv_size), BF16),
            pltpu.VMEM((BITS, count, kv_size), BF16),
            pltpu.VMEM((heads * SLOTS, count, HD), BF16),
            pltpu.VMEM((count, heads * EXPERTS * HD), BF16),
            pltpu.VMEM((2, count, slab), BF16),
            pltpu.VMEM((2, count, slab), BF16),
            pltpu.VMEM((count, slab), BF16),
            pltpu.VMEM((count, slab), BF16),
            pltpu.SemaphoreType.DMA,
            pltpu.SemaphoreType.DMA((2,)),
            pltpu.SemaphoreType.DMA((sends,)),
            pltpu.SemaphoreType.DMA((sends,)),
            pltpu.SemaphoreType.DMA((2, BITS)),
            pltpu.SemaphoreType.DMA((2, 3)),
        ],
        compiler_params=pltpu.CompilerParams(collective_id=0, has_side_effects=True),
        name="layer",
    )(tokens, gain[None, :], router, cols, rows, cosine, sine, shard)
    pages = page_shift.shape[0]
    return attended, cache.reshape(pages, count // pages, kv_size)


def solution(mesh):
    placed = (
        P("req", None),
        P("req", None),
        P("req"),
        P("req", None),
        P(),
        P(),
        P("req", "tensor"),
        P("req", "tensor"),
        P("tensor", "req"),
        P(),
    )
    return jax.shard_map(
        on_device,
        mesh=mesh,
        in_specs=placed,
        out_specs=(P("req", "tensor"), P("req", None, "tensor")),
        check_vma=False,
    )
```

```python
import functools

import jax
import jax.numpy as jnp
from jax import lax
from jax.experimental import pallas as pl
from jax.experimental.pallas import tpu as pltpu
from jax.sharding import PartitionSpec as P

HD = 128
EXPERTS = 4
SLOTS = 2
BITS = 4
MESH = pl.DeviceIdType.MESH
RING = 8
PAIR = 2
CORES = 2
HALF = RING // 2
REQ = RING * PAIR * RING
F32 = jnp.float32
BF16 = jnp.bfloat16


def place(z, x, y):
    return {"req": ((z + RING) % RING * PAIR + x) * RING + (y + RING) % RING}


def layer_kernel(
    parts,
    heads,
    tokens_ref,
    gain_ref,
    router_ref,
    cols_ref,
    seg_ref,
    pad_ref,
    cos_ref,
    sin_ref,
    kv_ref,
    wide_ref,
    out_ref,
    attended_ref,
    cache_ref,
    full_ref,
    normed_ref,
    bias_ref,
    gates_ref,
    stages_ref,
    inbox_ref,
    query_ref,
    mixed_ref,
    pair_out_ref,
    pair_in_ref,
    far_out_ref,
    far_in_ref,
    keep_sems,
    swap_sems,
    send_sems,
    recv_sems,
    page_sems,
    reduce_sems,
):
    count = tokens_ref.shape[0]
    me = lax.axis_index("req")
    z, x, y = me // (PAIR * RING), me // RING % PAIR, me % RING
    mine = lax.axis_index("tensor")
    low, core = mine // CORES, mine % CORES
    partner = place(z, 1 - x, y)
    core_mate = {"tensor": low * CORES + (1 - core)}
    far_mate = {"tensor": (1 - low) * CORES + core}
    around = {
        ("z", 1): place(z + 1, x, y),
        ("z", -1): place(z - 1, x, y),
        ("y", 1): place(z, x, y + 1),
        ("y", -1): place(z, x, y - 1),
    }
    levels = [2**level for level in reversed(range(BITS))]
    ahead = [{"req": (me + shift) % REQ} for shift in levels]
    behind = [{"req": (me + REQ - shift) % REQ} for shift in levels]

    barrier = pltpu.get_barrier_semaphore()
    greeted = [partner, core_mate, far_mate] + list(around.values()) + ahead + behind
    for device in greeted:
        pl.semaphore_signal(barrier, inc=1, device_id=device, device_id_type=MESH)
    pl.semaphore_wait(barrier, len(greeted))

    def remote(src, dst, send_sem, recv_sem, device):
        copy = pltpu.make_async_remote_copy(
            src_ref=src,
            dst_ref=dst,
            send_sem=send_sem,
            recv_sem=recv_sem,
            device_id=device,
            device_id_type=MESH,
        )
        copy.start()
        return copy

    (kv_first, kv_size), (query_first, query_size), (out_first, out_size) = parts
    begin, rest = pl.ds(0, out_first), pl.ds(out_first, out_size)
    keeps, swaps = [], []
    for index, (ref, (first, size)) in enumerate(zip((kv_ref, wide_ref, out_ref), parts)):
        here = full_ref.at[z, x, y, :, pl.ds(first, size)]
        swaps.append(remote(ref, here, swap_sems.at[0, index], swap_sems.at[1, index], partner))
        keep = pltpu.make_async_copy(ref, here, keep_sems.at[index])
        keep.start()
        keeps.append(keep)
    issued = []
    flying = {}

    def send(lane, block):
        axis, way = lane[0], lane[1]
        slot = len(issued)
        copy = remote(block, block, send_sems.at[slot], recv_sems.at[slot], around[axis, way])
        issued.append(copy)
        flying[lane] = copy

    def forward(step, hops, lane, block):
        if step < hops:
            if step > 0:
                flying[lane].wait_recv()
            send(lane, block)

    def first_round(step):
        for way in (1, -1):
            back = (-way) * step + RING
            hops = HALF if way == 1 else HALF - 1
            there = (y + back) % RING
            forward(step, hops, ("y", way, "whole"), full_ref.at[z, 1, there])
            forward(step, hops, ("z", way, "begin"), full_ref.at[(z + back) % RING, 0, y, :, begin])
            forward(step, hops, ("y", way, "rest"), full_ref.at[z, 0, there, :, rest])

    def first_turn(step, chunk):
        run = pl.ds(HALF * chunk, HALF)
        for way in (1, -1):
            back = (-way) * step + RING
            hops = HALF if (way == 1) == (chunk == 0) else HALF - 1
            forward(step, hops, ("z", way, 0, chunk), full_ref.at[(z + back) % RING, 1, run, :, begin])
            forward(step, hops, ("y", way, 0, chunk), full_ref.at[run, 0, (y + back) % RING, :, begin])

    def last_turn(step, chunk):
        run = pl.ds(HALF * (chunk // 2), HALF)
        for way in (1, -1):
            back = (-way) * step + RING
            hops = HALF if (way == 1) == (chunk % 2 == 0) else HALF - 1
            forward(
                step,
                hops,
                ("z", way, 1, chunk),
                full_ref.at[(z + back) % RING, chunk % 2, run, :, rest],
            )

    def arrived(kind):
        for lane, copy in flying.items():
            if lane[2] in kind:
                copy.wait_recv()

    def column(index):
        return cols_ref[:, index : index + 1]

    def rotate(values):
        return values * cos_ref[...] + pltpu.roll(values, HD // 2, 1) * sin_ref[...]

    def norm():
        block = 32
        for row in range(0, count, block):
            x_float = tokens_ref[row : row + block, :].astype(F32)
            scale = lax.rsqrt(jnp.mean(x_float * x_float, axis=1, keepdims=True) + 1e-06)
            normed = (x_float * scale * gain_ref[...]).astype(BF16)
            normed_ref[row : row + block, :] = normed
            normed = normed.astype(F32)
            logits = [
                jnp.sum(normed * router_ref[index : index + 1, :], axis=1, keepdims=True)
                for index in range(EXPERTS)
            ]
            for slot in range(SLOTS):
                expert = cols_ref[row : row + block, 2 + slot : 3 + slot]
                logit = jnp.zeros((block, 1), F32)
                for index in range(EXPERTS):
                    logit = logit + jnp.where(expert == index, logits[index], 0.0)
                gate = cols_ref[row : row + block, 1:2].astype(F32) / (1.0 + jnp.exp(-logit))
                gates_ref[slot, row : row + block, :] = jnp.broadcast_to(gate, (block, HD))

    def mask():
        query_index = lax.broadcasted_iota(jnp.int32, (count, count), 0)
        key_index = lax.broadcasted_iota(jnp.int32, (count, count), 1)
        same = (column(0) == seg_ref[...]) & (key_index <= query_index)
        allowed = same & ((pad_ref[...] == 1) | (key_index == query_index))
        bias_ref[...] = jnp.where(allowed, 0.0, -1e30)

    def weights_of(first, size):
        block = full_ref[:, :, :, :, first : first + size]
        return block.reshape(REQ * block.shape[3], size)

    def project_keys():
        first, size = parts[0]
        keyval = jnp.dot(normed_ref[...], weights_of(first, size), preferred_element_type=F32)
        padded = column(1).astype(F32)
        for head in range(heads):
            at = head * 2 * HD
            stages_ref[0, :, at : at + HD] = (rotate(keyval[:, at : at + HD]) * padded).astype(BF16)
            stages_ref[0, :, at + HD : at + 2 * HD] = (
                keyval[:, at + HD : at + 2 * HD] * padded
            ).astype(BF16)

    moves = []

    def page_send(level):
        moves.append(
            remote(
                stages_ref.at[level],
                inbox_ref.at[level],
                page_sems.at[0, level],
                page_sems.at[1, level],
                ahead[level],
            )
        )

    def page_take(level):
        moves[level].wait_recv()
        taken = column(4) // levels[level] % 2 == 1
        chosen = jnp.where(
            taken, inbox_ref[level].astype(F32), stages_ref[level].astype(F32)
        ).astype(BF16)
        if level == BITS - 1:
            cache_ref[...] = chosen
        else:
            stages_ref[level + 1] = chosen

    def project_queries(head):
        size = EXPERTS * HD
        every = jnp.dot(
            normed_ref[...], weights_of(parts[1][0] + head * size, size), preferred_element_type=F32
        )
        for slot in range(SLOTS):
            expert = column(2 + slot)
            chosen = jnp.zeros((count, HD), F32)
            for index in range(EXPERTS):
                chosen = chosen + jnp.where(
                    expert == index, every[:, index * HD : (index + 1) * HD], 0.0
                )
            query_ref[head * SLOTS + slot] = rotate(chosen).astype(BF16)

    def attend(head):
        at = head * 2 * HD
        keys = stages_ref[0, :, at : at + HD]
        values = stages_ref[0, :, at + HD : at + 2 * HD]
        outs = []
        for slot in range(SLOTS):
            scores = lax.dot_general(
                query_ref[head * SLOTS + slot],
                keys,
                (((1,), (1,)), ((), ())),
                preferred_element_type=F32,
            )
            masked = scores * (HD**-0.5) + bias_ref[...]
            weights = jnp.exp(masked - jnp.max(masked, axis=1, keepdims=True))
            total = jnp.sum(weights, axis=1, keepdims=True)
            summed = jnp.dot(weights.astype(BF16), values, preferred_element_type=F32)
            outs.append(summed / total * gates_ref[slot])
        for index in range(EXPERTS):
            mix = jnp.zeros((count, HD), F32)
            for slot in range(SLOTS):
                mix = mix + jnp.where(column(2 + slot) == index, outs[slot], 0.0)
            first = (head * EXPERTS + index) * HD
            mixed_ref[:, first : first + HD] = mix.astype(BF16)

    def project_out(owner):
        span = RING // (PAIR * CORES)
        first, size = parts[2]
        block = full_ref[pl.ds(owner * span, span), :, :, :, first : first + size]
        return lax.dot_general(
            mixed_ref[...],
            block.reshape(span * PAIR * RING * block.shape[3], size),
            (((1,), (1,)), ((), ())),
            preferred_element_type=F32,
        )

    norm()
    for copy in keeps + swaps:
        copy.wait()
    first_round(0)
    mask()
    for step in range(1, HALF):
        first_round(step)
    arrived(("whole", "begin", "rest"))
    for step in range(HALF):
        for chunk in (0, 1):
            first_turn(step, chunk)
    for chunk in range(4):
        last_turn(0, chunk)
    arrived((0,))
    project_keys()
    page_send(0)
    project_queries(0)
    last_turn(1, 0)
    last_turn(1, 1)
    project_queries(1)
    last_turn(1, 2)
    last_turn(1, 3)
    page_take(0)
    page_send(1)
    attend(0)
    last_turn(2, 0)
    last_turn(2, 1)
    attend(1)
    last_turn(2, 2)
    last_turn(2, 3)
    page_take(1)
    page_send(2)
    for chunk in range(4):
        last_turn(3, chunk)
    arrived((1,))
    page_take(2)
    page_send(3)

    def pair_send(index, owner):
        pair_out_ref[index] = project_out(owner).astype(BF16)
        return remote(
            pair_out_ref.at[index],
            pair_in_ref.at[index],
            reduce_sems.at[0, index],
            reduce_sems.at[1, index],
            core_mate,
        )

    pairs = [pair_send(0, (1 - low) * CORES + (1 - core))]
    far = project_out((1 - low) * CORES + core)
    pairs[0].wait_recv()
    far_out_ref[...] = (far + pair_in_ref[0].astype(F32)).astype(BF16)
    far_copy = remote(far_out_ref, far_in_ref, reduce_sems.at[0, 2], reduce_sems.at[1, 2], far_mate)
    pairs.append(pair_send(1, low * CORES + (1 - core)))
    near = project_out(low * CORES + core)
    pairs[1].wait_recv()
    near = near + pair_in_ref[1].astype(F32)
    page_take(3)
    far_copy.wait_recv()
    attended_ref[...] = (near + far_in_ref[...].astype(F32)).astype(BF16)

    for copy in issued + moves + pairs + [far_copy]:
        copy.wait_send()


def on_device(
    tokens, segment_ids, padding, attn_experts, gain, w_router, w_query, w_kv, w_out, page_shift
):
    count, width = tokens.shape
    seg_row = segment_ids[0]
    starts = jnp.sum((seg_row[None, :] < seg_row[:, None]).astype(jnp.int32), axis=1)
    position = jnp.arange(count, dtype=jnp.int32) - starts
    half_size = HD // 2
    freqs = 10000.0 ** (-jnp.arange(half_size, dtype=F32) / half_size)
    angles = position.astype(F32)[:, None] * freqs[None, :]
    cosine, sine = jnp.cos(angles), jnp.sin(angles)
    cosine = jnp.concatenate([cosine, cosine], axis=1)
    sine = jnp.concatenate([-sine, sine], axis=1)
    shifts = jnp.repeat(page_shift, count // page_shift.shape[0])
    cols = jnp.stack([seg_row, padding, attn_experts[:, 0], attn_experts[:, 1], shifts], axis=1)
    kv_size, query_size, out_size = w_kv.shape[1], w_query.shape[1], w_out.shape[0]
    parts = ((0, kv_size), (kv_size, query_size), (kv_size + query_size, out_size))
    heads = kv_size // (2 * HD)
    slab = width // (PAIR * CORES)
    sends = 3 * (2 * HALF - 1) + 2 * (8 * HALF - 4)
    depth = w_kv.shape[0]
    vmem = pl.BlockSpec(memory_space=pltpu.VMEM)
    attended, cache = pl.pallas_call(
        functools.partial(layer_kernel, parts, heads),
        out_shape=(
            jax.ShapeDtypeStruct((count, slab), BF16),
            jax.ShapeDtypeStruct((count, kv_size), BF16),
        ),
        in_specs=[vmem] * 8 + [pl.BlockSpec(memory_space=pl.ANY)] * 3,
        out_specs=(vmem, vmem),
        scratch_shapes=[
            pltpu.VMEM((RING, PAIR, RING, depth, kv_size + query_size + out_size), BF16),
            pltpu.VMEM((count, width), BF16),
            pltpu.VMEM((count, count), F32),
            pltpu.VMEM((SLOTS, count, HD), F32),
            pltpu.VMEM((BITS, count, kv_size), BF16),
            pltpu.VMEM((BITS, count, kv_size), BF16),
            pltpu.VMEM((heads * SLOTS, count, HD), BF16),
            pltpu.VMEM((count, heads * EXPERTS * HD), BF16),
            pltpu.VMEM((2, count, slab), BF16),
            pltpu.VMEM((2, count, slab), BF16),
            pltpu.VMEM((count, slab), BF16),
            pltpu.VMEM((count, slab), BF16),
            pltpu.SemaphoreType.DMA((3,)),
            pltpu.SemaphoreType.DMA((2, 3)),
            pltpu.SemaphoreType.DMA((sends,)),
            pltpu.SemaphoreType.DMA((sends,)),
            pltpu.SemaphoreType.DMA((2, BITS)),
            pltpu.SemaphoreType.DMA((2, 3)),
        ],
        compiler_params=pltpu.CompilerParams(collective_id=0, has_side_effects=True),
        name="layer",
    )(
        tokens,
        gain[None, :],
        w_router.T,
        cols,
        segment_ids,
        padding[None, :],
        cosine,
        sine,
        w_kv,
        w_query,
        w_out.T,
    )
    pages = page_shift.shape[0]
    return attended, cache.reshape(pages, count // pages, kv_size)


def solution(mesh):
    placed = (
        P("req", None),
        P("req", None),
        P("req"),
        P("req", None),
        P(),
        P(),
        P("req", "tensor"),
        P("req", "tensor"),
        P("tensor", "req"),
        P(),
    )
    return jax.shard_map(
        on_device,
        mesh=mesh,
        in_specs=placed,
        out_specs=(P("req", "tensor"), P("req", None, "tensor")),
        check_vma=False,
    )
```

```python
import functools

import jax
import jax.numpy as jnp
from jax import lax
from jax.experimental import pallas as pl
from jax.experimental.pallas import tpu as pltpu
from jax.sharding import PartitionSpec as P

HD = 128
EXPERTS = 4
SLOTS = 2
BITS = 4
MESH = pl.DeviceIdType.MESH
RING = 8
PAIR = 2
CORES = 2
HALF = RING // 2
REQ = RING * PAIR * RING
F32 = jnp.float32
BF16 = jnp.bfloat16


def place(z, x, y):
    return {"req": ((z + RING) % RING * PAIR + x) * RING + (y + RING) % RING}


def layer_kernel(
    parts,
    heads,
    tokens_ref,
    gain_ref,
    router_ref,
    cols_ref,
    seg_ref,
    pad_ref,
    cos_ref,
    sin_ref,
    kv_ref,
    wide_ref,
    out_ref,
    attended_ref,
    cache_ref,
    full_ref,
    normed_ref,
    bias_ref,
    gates_ref,
    stages_ref,
    inbox_ref,
    query_ref,
    mixed_ref,
    pair_out_ref,
    pair_in_ref,
    far_out_ref,
    far_in_ref,
    keep_sems,
    swap_sems,
    send_sems,
    recv_sems,
    page_sems,
    reduce_sems,
):
    count = tokens_ref.shape[0]
    me = lax.axis_index("req")
    z, x, y = me // (PAIR * RING), me // RING % PAIR, me % RING
    mine = lax.axis_index("tensor")
    low, core = mine // CORES, mine % CORES
    partner = place(z, 1 - x, y)
    core_mate = {"tensor": low * CORES + (1 - core)}
    far_mate = {"tensor": (1 - low) * CORES + core}
    around = {
        ("z", 1): place(z + 1, x, y),
        ("z", -1): place(z - 1, x, y),
        ("y", 1): place(z, x, y + 1),
        ("y", -1): place(z, x, y - 1),
    }
    levels = [2**level for level in reversed(range(BITS))]
    ahead = [{"req": (me + shift) % REQ} for shift in levels]
    behind = [{"req": (me + REQ - shift) % REQ} for shift in levels]

    barrier = pltpu.get_barrier_semaphore()
    greeted = [partner, core_mate, far_mate] + list(around.values()) + ahead + behind
    for device in greeted:
        pl.semaphore_signal(barrier, inc=1, device_id=device, device_id_type=MESH)
    pl.semaphore_wait(barrier, len(greeted))

    def remote(src, dst, send_sem, recv_sem, device):
        copy = pltpu.make_async_remote_copy(
            src_ref=src,
            dst_ref=dst,
            send_sem=send_sem,
            recv_sem=recv_sem,
            device_id=device,
            device_id_type=MESH,
        )
        copy.start()
        return copy

    keeps, swaps = [], []
    for index, (ref, (first, size)) in enumerate(zip((kv_ref, wide_ref, out_ref), parts)):
        here = full_ref.at[z, x, y, :, pl.ds(first, size)]
        swaps.append(remote(ref, here, swap_sems.at[0, index], swap_sems.at[1, index], partner))
        keep = pltpu.make_async_copy(ref, here, keep_sems.at[index])
        keep.start()
        keeps.append(keep)
    groups = ((0, parts[2][0]), parts[2])
    issued = []

    def send(axis, way, block):
        slot = len(issued)
        copy = remote(block, block, send_sems.at[slot], recv_sems.at[slot], around[axis, way])
        issued.append(copy)
        return copy

    def single(axis, way, step):
        back = (-way) * step + RING
        if axis == "z":
            return full_ref.at[(z + back) % RING, 0, y]
        return full_ref.at[z, 1, (y + back) % RING]

    def several(axis, way, step, part, chunk):
        back = (-way) * step + RING
        columns = pl.ds(*groups[part])
        run = pl.ds(HALF * chunk, HALF)
        if axis == "y":
            return full_ref.at[run, 0, (y + back) % RING, :, columns]
        return full_ref.at[(z + back) % RING, 1, run, :, columns]

    flying = {}
    streams = [(axis, way) for way in (1, -1) for axis in ("z", "y")]

    def first_round(step):
        for axis, way in streams:
            if step < (HALF if way == 1 else HALF - 1):
                if step > 0:
                    flying[axis, way].wait_recv()
                flying[axis, way] = send(axis, way, single(axis, way, step))

    def first_end():
        for stream in streams:
            flying[stream].wait_recv()

    def turn(part, step, chunk):
        for axis, way in streams:
            if step < (HALF if (way == 1) == (chunk == 0) else HALF - 1):
                lane = (axis, way, part, chunk)
                if step > 0:
                    flying[lane].wait_recv()
                flying[lane] = send(axis, way, several(axis, way, step, part, chunk))

    def arrived(part):
        for chunk in (0, 1):
            for axis, way in streams:
                flying[axis, way, part, chunk].wait_recv()

    def column(index):
        return cols_ref[:, index : index + 1]

    def rotate(values):
        return values * cos_ref[...] + pltpu.roll(values, HD // 2, 1) * sin_ref[...]

    def norm():
        block = 32
        for row in range(0, count, block):
            x_float = tokens_ref[row : row + block, :].astype(F32)
            scale = lax.rsqrt(jnp.mean(x_float * x_float, axis=1, keepdims=True) + 1e-06)
            normed = (x_float * scale * gain_ref[...]).astype(BF16)
            normed_ref[row : row + block, :] = normed
            normed = normed.astype(F32)
            logits = [
                jnp.sum(normed * router_ref[index : index + 1, :], axis=1, keepdims=True)
                for index in range(EXPERTS)
            ]
            for slot in range(SLOTS):
                expert = cols_ref[row : row + block, 2 + slot : 3 + slot]
                logit = jnp.zeros((block, 1), F32)
                for index in range(EXPERTS):
                    logit = logit + jnp.where(expert == index, logits[index], 0.0)
                gate = cols_ref[row : row + block, 1:2].astype(F32) / (1.0 + jnp.exp(-logit))
                gates_ref[slot, row : row + block, :] = jnp.broadcast_to(gate, (block, HD))

    def mask():
        query_index = lax.broadcasted_iota(jnp.int32, (count, count), 0)
        key_index = lax.broadcasted_iota(jnp.int32, (count, count), 1)
        same = (column(0) == seg_ref[...]) & (key_index <= query_index)
        allowed = same & ((pad_ref[...] == 1) | (key_index == query_index))
        bias_ref[...] = jnp.where(allowed, 0.0, -1e30)

    def weights_of(first, size):
        block = full_ref[:, :, :, :, first : first + size]
        return block.reshape(REQ * block.shape[3], size)

    def project_keys():
        first, size = parts[0]
        keyval = jnp.dot(normed_ref[...], weights_of(first, size), preferred_element_type=F32)
        padded = column(1).astype(F32)
        for head in range(heads):
            at = head * 2 * HD
            stages_ref[0, :, at : at + HD] = (rotate(keyval[:, at : at + HD]) * padded).astype(BF16)
            stages_ref[0, :, at + HD : at + 2 * HD] = (
                keyval[:, at + HD : at + 2 * HD] * padded
            ).astype(BF16)

    moves = []

    def page_send(level):
        moves.append(
            remote(
                stages_ref.at[level],
                inbox_ref.at[level],
                page_sems.at[0, level],
                page_sems.at[1, level],
                ahead[level],
            )
        )

    def page_take(level):
        moves[level].wait_recv()
        taken = column(4) // levels[level] % 2 == 1
        chosen = jnp.where(
            taken, inbox_ref[level].astype(F32), stages_ref[level].astype(F32)
        ).astype(BF16)
        if level == BITS - 1:
            cache_ref[...] = chosen
        else:
            stages_ref[level + 1] = chosen

    def project_queries(head):
        size = EXPERTS * HD
        every = jnp.dot(
            normed_ref[...], weights_of(parts[1][0] + head * size, size), preferred_element_type=F32
        )
        for slot in range(SLOTS):
            expert = column(2 + slot)
            chosen = jnp.zeros((count, HD), F32)
            for index in range(EXPERTS):
                chosen = chosen + jnp.where(
                    expert == index, every[:, index * HD : (index + 1) * HD], 0.0
                )
            query_ref[head * SLOTS + slot] = rotate(chosen).astype(BF16)

    def attend(head):
        at = head * 2 * HD
        keys = stages_ref[0, :, at : at + HD]
        values = stages_ref[0, :, at + HD : at + 2 * HD]
        outs = []
        for slot in range(SLOTS):
            scores = lax.dot_general(
                query_ref[head * SLOTS + slot],
                keys,
                (((1,), (1,)), ((), ())),
                preferred_element_type=F32,
            )
            masked = scores * (HD**-0.5) + bias_ref[...]
            weights = jnp.exp(masked - jnp.max(masked, axis=1, keepdims=True))
            total = jnp.sum(weights, axis=1, keepdims=True)
            summed = jnp.dot(weights.astype(BF16), values, preferred_element_type=F32)
            outs.append(summed / total * gates_ref[slot])
        for index in range(EXPERTS):
            mix = jnp.zeros((count, HD), F32)
            for slot in range(SLOTS):
                mix = mix + jnp.where(column(2 + slot) == index, outs[slot], 0.0)
            first = (head * EXPERTS + index) * HD
            mixed_ref[:, first : first + HD] = mix.astype(BF16)

    def project_out(owner):
        span = RING // (PAIR * CORES)
        first, size = parts[2]
        block = full_ref[pl.ds(owner * span, span), :, :, :, first : first + size]
        return lax.dot_general(
            mixed_ref[...],
            block.reshape(span * PAIR * RING * block.shape[3], size),
            (((1,), (1,)), ((), ())),
            preferred_element_type=F32,
        )

    norm()
    for copy in keeps + swaps:
        copy.wait()
    first_round(0)
    mask()
    first_round(1)
    for step in (2, 3):
        first_round(step)
    first_end()
    for step in range(HALF):
        for chunk in (0, 1):
            turn(0, step, chunk)
    turn(1, 0, 0)
    turn(1, 0, 1)
    arrived(0)
    project_keys()
    page_send(0)
    project_queries(0)
    turn(1, 1, 0)
    turn(1, 1, 1)
    project_queries(1)
    page_take(0)
    page_send(1)
    attend(0)
    turn(1, 2, 0)
    turn(1, 2, 1)
    attend(1)
    turn(1, 3, 0)
    turn(1, 3, 1)
    page_take(1)
    page_send(2)
    arrived(1)

    def pair_send(index, owner):
        pair_out_ref[index] = project_out(owner).astype(BF16)
        return remote(
            pair_out_ref.at[index],
            pair_in_ref.at[index],
            reduce_sems.at[0, index],
            reduce_sems.at[1, index],
            core_mate,
        )

    pairs = [pair_send(0, (1 - low) * CORES + (1 - core))]
    far = project_out((1 - low) * CORES + core)
    pairs[0].wait_recv()
    far_out_ref[...] = (far + pair_in_ref[0].astype(F32)).astype(BF16)
    far_copy = remote(far_out_ref, far_in_ref, reduce_sems.at[0, 2], reduce_sems.at[1, 2], far_mate)
    pairs.append(pair_send(1, low * CORES + (1 - core)))
    near = project_out(low * CORES + core)
    pairs[1].wait_recv()
    near = near + pair_in_ref[1].astype(F32)
    page_take(2)
    page_send(3)
    far_copy.wait_recv()
    attended_ref[...] = (near + far_in_ref[...].astype(F32)).astype(BF16)

    page_take(3)
    for copy in issued + moves + pairs + [far_copy]:
        copy.wait_send()


def on_device(
    tokens, segment_ids, padding, attn_experts, gain, w_router, w_query, w_kv, w_out, page_shift
):
    count, width = tokens.shape
    seg_row = segment_ids[0]
    starts = jnp.sum((seg_row[None, :] < seg_row[:, None]).astype(jnp.int32), axis=1)
    position = jnp.arange(count, dtype=jnp.int32) - starts
    half_size = HD // 2
    freqs = 10000.0 ** (-jnp.arange(half_size, dtype=F32) / half_size)
    angles = position.astype(F32)[:, None] * freqs[None, :]
    cosine, sine = jnp.cos(angles), jnp.sin(angles)
    cosine = jnp.concatenate([cosine, cosine], axis=1)
    sine = jnp.concatenate([-sine, sine], axis=1)
    shifts = jnp.repeat(page_shift, count // page_shift.shape[0])
    cols = jnp.stack([seg_row, padding, attn_experts[:, 0], attn_experts[:, 1], shifts], axis=1)
    kv_size, query_size, out_size = w_kv.shape[1], w_query.shape[1], w_out.shape[0]
    parts = ((0, kv_size), (kv_size, query_size), (kv_size + query_size, out_size))
    heads = kv_size // (2 * HD)
    depth = w_kv.shape[0]
    slab = width // (PAIR * CORES)
    sends = (4 * HALF - 2) + 2 * (8 * HALF - 4)
    vmem = pl.BlockSpec(memory_space=pltpu.VMEM)
    attended, cache = pl.pallas_call(
        functools.partial(layer_kernel, parts, heads),
        out_shape=(
            jax.ShapeDtypeStruct((count, slab), BF16),
            jax.ShapeDtypeStruct((count, kv_size), BF16),
        ),
        in_specs=[vmem] * 8 + [pl.BlockSpec(memory_space=pl.ANY)] * 3,
        out_specs=(vmem, vmem),
        scratch_shapes=[
            pltpu.VMEM((RING, PAIR, RING, depth, kv_size + query_size + out_size), BF16),
            pltpu.VMEM((count, width), BF16),
            pltpu.VMEM((count, count), F32),
            pltpu.VMEM((SLOTS, count, HD), F32),
            pltpu.VMEM((BITS, count, kv_size), BF16),
            pltpu.VMEM((BITS, count, kv_size), BF16),
            pltpu.VMEM((heads * SLOTS, count, HD), BF16),
            pltpu.VMEM((count, heads * EXPERTS * HD), BF16),
            pltpu.VMEM((2, count, slab), BF16),
            pltpu.VMEM((2, count, slab), BF16),
            pltpu.VMEM((count, slab), BF16),
            pltpu.VMEM((count, slab), BF16),
            pltpu.SemaphoreType.DMA((3,)),
            pltpu.SemaphoreType.DMA((2, 3)),
            pltpu.SemaphoreType.DMA((sends,)),
            pltpu.SemaphoreType.DMA((sends,)),
            pltpu.SemaphoreType.DMA((2, BITS)),
            pltpu.SemaphoreType.DMA((2, 3)),
        ],
        compiler_params=pltpu.CompilerParams(collective_id=0, has_side_effects=True),
        name="layer",
    )(
        tokens,
        gain[None, :],
        w_router.T,
        cols,
        segment_ids,
        padding[None, :],
        cosine,
        sine,
        w_kv,
        w_query,
        w_out.T,
    )
    pages = page_shift.shape[0]
    return attended, cache.reshape(pages, count // pages, kv_size)


def solution(mesh):
    placed = (
        P("req", None),
        P("req", None),
        P("req"),
        P("req", None),
        P(),
        P(),
        P("req", "tensor"),
        P("req", "tensor"),
        P("tensor", "req"),
        P(),
    )
    return jax.shard_map(
        on_device,
        mesh=mesh,
        in_specs=placed,
        out_specs=(P("req", "tensor"), P("req", None, "tensor")),
        check_vma=False,
    )
```

```python
import functools

import jax
import jax.numpy as jnp
from jax import lax
from jax.experimental import pallas as pl
from jax.experimental.pallas import tpu as pltpu
from jax.sharding import PartitionSpec as P

HD = 128
EXPERTS = 4
SLOTS = 2
BITS = 4
MESH = pl.DeviceIdType.MESH
RING = 8
PAIR = 2
CORES = 2
HALF = RING // 2
REQ = RING * PAIR * RING
F32 = jnp.float32
BF16 = jnp.bfloat16


def place(z, x, y):
    return {"req": ((z + RING) % RING * PAIR + x) * RING + (y + RING) % RING}


def layer_kernel(
    parts,
    heads,
    tokens_ref,
    gain_ref,
    router_ref,
    cols_ref,
    seg_ref,
    pad_ref,
    cos_ref,
    sin_ref,
    kv_ref,
    wide_ref,
    out_ref,
    attended_ref,
    cache_ref,
    full_ref,
    normed_ref,
    bias_ref,
    gates_ref,
    stages_ref,
    inbox_ref,
    query_ref,
    mixed_ref,
    pair_out_ref,
    pair_in_ref,
    far_out_ref,
    far_in_ref,
    keep_sems,
    swap_sems,
    send_sems,
    recv_sems,
    page_sems,
    reduce_sems,
):
    count = tokens_ref.shape[0]
    me = lax.axis_index("req")
    z, x, y = me // (PAIR * RING), me // RING % PAIR, me % RING
    mine = lax.axis_index("tensor")
    low, core = mine // CORES, mine % CORES
    partner = place(z, 1 - x, y)
    core_mate = {"tensor": low * CORES + (1 - core)}
    far_mate = {"tensor": (1 - low) * CORES + core}
    around = {
        ("z", 1): place(z + 1, x, y),
        ("z", -1): place(z - 1, x, y),
        ("y", 1): place(z, x, y + 1),
        ("y", -1): place(z, x, y - 1),
    }
    levels = [2, 4, 8, 1]
    ahead = [{"req": (me + shift) % REQ} for shift in levels]
    behind = [{"req": (me + REQ - shift) % REQ} for shift in levels]

    barrier = pltpu.get_barrier_semaphore()
    greeted = [partner, core_mate, far_mate] + list(around.values()) + ahead + behind
    for device in greeted:
        pl.semaphore_signal(barrier, inc=1, device_id=device, device_id_type=MESH)
    pl.semaphore_wait(barrier, len(greeted))

    def remote(src, dst, send_sem, recv_sem, device):
        copy = pltpu.make_async_remote_copy(
            src_ref=src,
            dst_ref=dst,
            send_sem=send_sem,
            recv_sem=recv_sem,
            device_id=device,
            device_id_type=MESH,
        )
        copy.start()
        return copy

    keeps, swaps = [], []
    for index, (ref, (first, size)) in enumerate(zip((kv_ref, wide_ref, out_ref), parts)):
        here = full_ref.at[z, x, y, :, pl.ds(first, size)]
        swaps.append(remote(ref, here, swap_sems.at[0, index], swap_sems.at[1, index], partner))
        keep = pltpu.make_async_copy(ref, here, keep_sems.at[index])
        keep.start()
        keeps.append(keep)
    groups = ((0, parts[2][0]), parts[2])
    issued = []

    def send(axis, way, block):
        slot = len(issued)
        copy = remote(block, block, send_sems.at[slot], recv_sems.at[slot], around[axis, way])
        issued.append(copy)
        return copy

    def single(axis, way, step):
        back = (-way) * step + RING
        if axis == "z":
            return full_ref.at[(z + back) % RING, 0, y]
        return full_ref.at[z, 1, (y + back) % RING]

    def several(axis, way, step, part, chunk):
        back = (-way) * step + RING
        columns = pl.ds(*groups[part])
        run = pl.ds(HALF * chunk, HALF)
        if axis == "y":
            return full_ref.at[run, 0, (y + back) % RING, :, columns]
        return full_ref.at[(z + back) % RING, 1, run, :, columns]

    flying = {}
    streams = [(axis, way) for way in (1, -1) for axis in ("z", "y")]

    def first_round(step):
        for axis, way in streams:
            if step < (HALF if way == 1 else HALF - 1):
                if step > 0:
                    flying[axis, way].wait_recv()
                flying[axis, way] = send(axis, way, single(axis, way, step))

    def first_end():
        for stream in streams:
            flying[stream].wait_recv()

    def turn(part, step, chunk):
        for axis, way in streams:
            if step < (HALF if (way == 1) == (chunk == 0) else HALF - 1):
                lane = (axis, way, part, chunk)
                if step > 0:
                    flying[lane].wait_recv()
                flying[lane] = send(axis, way, several(axis, way, step, part, chunk))

    def arrived(part):
        for chunk in (0, 1):
            for axis, way in streams:
                flying[axis, way, part, chunk].wait_recv()

    def column(index):
        return cols_ref[:, index : index + 1]

    def rotate(values):
        return values * cos_ref[...] + pltpu.roll(values, HD // 2, 1) * sin_ref[...]

    def norm():
        block = 32
        for row in range(0, count, block):
            x_float = tokens_ref[row : row + block, :].astype(F32)
            scale = lax.rsqrt(jnp.mean(x_float * x_float, axis=1, keepdims=True) + 1e-06)
            normed = (x_float * scale * gain_ref[...]).astype(BF16)
            normed_ref[row : row + block, :] = normed
            normed = normed.astype(F32)
            logits = [
                jnp.sum(normed * router_ref[index : index + 1, :], axis=1, keepdims=True)
                for index in range(EXPERTS)
            ]
            for slot in range(SLOTS):
                expert = cols_ref[row : row + block, 2 + slot : 3 + slot]
                logit = jnp.zeros((block, 1), F32)
                for index in range(EXPERTS):
                    logit = logit + jnp.where(expert == index, logits[index], 0.0)
                gate = cols_ref[row : row + block, 1:2].astype(F32) / (1.0 + jnp.exp(-logit))
                gates_ref[slot, row : row + block, :] = jnp.broadcast_to(gate, (block, HD))

    def mask():
        query_index = lax.broadcasted_iota(jnp.int32, (count, count), 0)
        key_index = lax.broadcasted_iota(jnp.int32, (count, count), 1)
        same = (column(0) == seg_ref[...]) & (key_index <= query_index)
        allowed = same & ((pad_ref[...] == 1) | (key_index == query_index))
        bias_ref[...] = jnp.where(allowed, 0.0, -1e30)

    def weights_of(first, size):
        block = full_ref[:, :, :, :, first : first + size]
        return block.reshape(REQ * block.shape[3], size)

    def project_keys():
        first, size = parts[0]
        keyval = jnp.dot(normed_ref[...], weights_of(first, size), preferred_element_type=F32)
        padded = column(1).astype(F32)
        for head in range(heads):
            at = head * 2 * HD
            stages_ref[0, :, at : at + HD] = (rotate(keyval[:, at : at + HD]) * padded).astype(BF16)
            stages_ref[0, :, at + HD : at + 2 * HD] = (
                keyval[:, at + HD : at + 2 * HD] * padded
            ).astype(BF16)

    moves = []

    def page_send(level):
        moves.append(
            remote(
                stages_ref.at[level],
                inbox_ref.at[level],
                page_sems.at[0, level],
                page_sems.at[1, level],
                ahead[level],
            )
        )

    def page_take(level):
        moves[level].wait_recv()
        taken = column(4) // levels[level] % 2 == 1
        chosen = jnp.where(
            taken, inbox_ref[level].astype(F32), stages_ref[level].astype(F32)
        ).astype(BF16)
        if level == BITS - 1:
            cache_ref[...] = chosen
        else:
            stages_ref[level + 1] = chosen

    def project_queries(head):
        size = EXPERTS * HD
        every = jnp.dot(
            normed_ref[...], weights_of(parts[1][0] + head * size, size), preferred_element_type=F32
        )
        for slot in range(SLOTS):
            expert = column(2 + slot)
            chosen = jnp.zeros((count, HD), F32)
            for index in range(EXPERTS):
                chosen = chosen + jnp.where(
                    expert == index, every[:, index * HD : (index + 1) * HD], 0.0
                )
            query_ref[head * SLOTS + slot] = rotate(chosen).astype(BF16)

    def attend(head):
        at = head * 2 * HD
        keys = stages_ref[0, :, at : at + HD]
        values = stages_ref[0, :, at + HD : at + 2 * HD]
        outs = []
        for slot in range(SLOTS):
            scores = lax.dot_general(
                query_ref[head * SLOTS + slot],
                keys,
                (((1,), (1,)), ((), ())),
                preferred_element_type=F32,
            )
            masked = scores * (HD**-0.5) + bias_ref[...]
            weights = jnp.exp(masked - jnp.max(masked, axis=1, keepdims=True))
            total = jnp.sum(weights, axis=1, keepdims=True)
            summed = jnp.dot(weights.astype(BF16), values, preferred_element_type=F32)
            outs.append(summed / total * gates_ref[slot])
        for index in range(EXPERTS):
            mix = jnp.zeros((count, HD), F32)
            for slot in range(SLOTS):
                mix = mix + jnp.where(column(2 + slot) == index, outs[slot], 0.0)
            first = (head * EXPERTS + index) * HD
            mixed_ref[:, first : first + HD] = mix.astype(BF16)

    def project_out(owner):
        span = RING // (PAIR * CORES)
        first, size = parts[2]
        block = full_ref[pl.ds(owner * span, span), :, :, :, first : first + size]
        return lax.dot_general(
            mixed_ref[...],
            block.reshape(span * PAIR * RING * block.shape[3], size),
            (((1,), (1,)), ((), ())),
            preferred_element_type=F32,
        )

    norm()
    for copy in keeps + swaps:
        copy.wait()
    first_round(0)
    mask()
    first_round(1)
    for step in (2, 3):
        first_round(step)
    first_end()
    for step in range(HALF):
        for chunk in (0, 1):
            turn(0, step, chunk)
    turn(1, 0, 0)
    turn(1, 0, 1)
    arrived(0)
    project_keys()
    page_send(0)
    project_queries(0)
    turn(1, 1, 0)
    turn(1, 1, 1)
    project_queries(1)
    page_take(0)
    page_send(1)
    attend(0)
    turn(1, 2, 0)
    turn(1, 2, 1)
    attend(1)
    turn(1, 3, 0)
    turn(1, 3, 1)
    page_take(1)
    page_send(2)
    arrived(1)

    def pair_send(index, owner):
        pair_out_ref[index] = project_out(owner).astype(BF16)
        return remote(
            pair_out_ref.at[index],
            pair_in_ref.at[index],
            reduce_sems.at[0, index],
            reduce_sems.at[1, index],
            core_mate,
        )

    pairs = [pair_send(0, (1 - low) * CORES + (1 - core))]
    far = project_out((1 - low) * CORES + core)
    pairs[0].wait_recv()
    far_out_ref[...] = (far + pair_in_ref[0].astype(F32)).astype(BF16)
    far_copy = remote(far_out_ref, far_in_ref, reduce_sems.at[0, 2], reduce_sems.at[1, 2], far_mate)
    pairs.append(pair_send(1, low * CORES + (1 - core)))
    near = project_out(low * CORES + core)
    pairs[1].wait_recv()
    near = near + pair_in_ref[1].astype(F32)
    page_take(2)
    page_send(3)
    far_copy.wait_recv()
    attended_ref[...] = (near + far_in_ref[...].astype(F32)).astype(BF16)

    page_take(3)
    for copy in issued + moves + pairs + [far_copy]:
        copy.wait_send()


def on_device(
    tokens, segment_ids, padding, attn_experts, gain, w_router, w_query, w_kv, w_out, page_shift
):
    count, width = tokens.shape
    seg_row = segment_ids[0]
    starts = jnp.sum((seg_row[None, :] < seg_row[:, None]).astype(jnp.int32), axis=1)
    position = jnp.arange(count, dtype=jnp.int32) - starts
    half_size = HD // 2
    freqs = 10000.0 ** (-jnp.arange(half_size, dtype=F32) / half_size)
    angles = position.astype(F32)[:, None] * freqs[None, :]
    cosine, sine = jnp.cos(angles), jnp.sin(angles)
    cosine = jnp.concatenate([cosine, cosine], axis=1)
    sine = jnp.concatenate([-sine, sine], axis=1)
    shifts = jnp.repeat(page_shift, count // page_shift.shape[0])
    cols = jnp.stack([seg_row, padding, attn_experts[:, 0], attn_experts[:, 1], shifts], axis=1)
    kv_size, query_size, out_size = w_kv.shape[1], w_query.shape[1], w_out.shape[0]
    parts = ((0, kv_size), (kv_size, query_size), (kv_size + query_size, out_size))
    heads = kv_size // (2 * HD)
    depth = w_kv.shape[0]
    slab = width // (PAIR * CORES)
    sends = (4 * HALF - 2) + 2 * (8 * HALF - 4)
    vmem = pl.BlockSpec(memory_space=pltpu.VMEM)
    attended, cache = pl.pallas_call(
        functools.partial(layer_kernel, parts, heads),
        out_shape=(
            jax.ShapeDtypeStruct((count, slab), BF16),
            jax.ShapeDtypeStruct((count, kv_size), BF16),
        ),
        in_specs=[vmem] * 8 + [pl.BlockSpec(memory_space=pl.ANY)] * 3,
        out_specs=(vmem, vmem),
        scratch_shapes=[
            pltpu.VMEM((RING, PAIR, RING, depth, kv_size + query_size + out_size), BF16),
            pltpu.VMEM((count, width), BF16),
            pltpu.VMEM((count, count), F32),
            pltpu.VMEM((SLOTS, count, HD), F32),
            pltpu.VMEM((BITS, count, kv_size), BF16),
            pltpu.VMEM((BITS, count, kv_size), BF16),
            pltpu.VMEM((heads * SLOTS, count, HD), BF16),
            pltpu.VMEM((count, heads * EXPERTS * HD), BF16),
            pltpu.VMEM((2, count, slab), BF16),
            pltpu.VMEM((2, count, slab), BF16),
            pltpu.VMEM((count, slab), BF16),
            pltpu.VMEM((count, slab), BF16),
            pltpu.SemaphoreType.DMA((3,)),
            pltpu.SemaphoreType.DMA((2, 3)),
            pltpu.SemaphoreType.DMA((sends,)),
            pltpu.SemaphoreType.DMA((sends,)),
            pltpu.SemaphoreType.DMA((2, BITS)),
            pltpu.SemaphoreType.DMA((2, 3)),
        ],
        compiler_params=pltpu.CompilerParams(collective_id=0, has_side_effects=True),
        name="layer",
    )(
        tokens,
        gain[None, :],
        w_router.T,
        cols,
        segment_ids,
        padding[None, :],
        cosine,
        sine,
        w_kv,
        w_query,
        w_out.T,
    )
    pages = page_shift.shape[0]
    return attended, cache.reshape(pages, count // pages, kv_size)


def solution(mesh):
    placed = (
        P("req", None),
        P("req", None),
        P("req"),
        P("req", None),
        P(),
        P(),
        P("req", "tensor"),
        P("req", "tensor"),
        P("tensor", "req"),
        P(),
    )
    return jax.shard_map(
        on_device,
        mesh=mesh,
        in_specs=placed,
        out_specs=(P("req", "tensor"), P("req", None, "tensor")),
        check_vma=False,
    )
```
